32 devices in a mesh: group: 2 (over x), patch: 16 (over z, y, core).
Axes of the slice: x: 2, y: 2, z: 4, core: 2. Of those that a mesh axis runs over, the one named last changes fastest.
Arguments:
- queries: bfloat16 [1024, 1536], P(('group', 'patch')), parts along dimension 0, may hold values from -6 to 6
- keys: bfloat16 [1024, 1536], P(('group', 'patch')), parts along dimension 0, may hold values from -6 to 6
- values: bfloat16 [1024, 1536], P(('group', 'patch')), parts along dimension 0, may hold values from -6 to 6
- stale_keys: bfloat16 [1024, 1536], P(('group', 'patch')), parts along dimension 0, may hold values from -6 to 6
- stale_values: bfloat16 [1024, 1536], P(('group', 'patch')), parts along dimension 0, may hold values from -6 to 6
- text_keys: bfloat16 [32, 512, 1536], P(('group', 'patch')), parts along dimension 0, may hold values from -200 to 200
- text_values: bfloat16 [32, 512, 1536], P(('group', 'patch')), parts along dimension 0, may hold values from -6 to 6
- prompt_device: int32 [2], P('group'), parts along dimension 0, may hold values from 0 to 15
- patch_owner: int32 [32], P('group'), parts along dimension 0, may hold values from 0 to 15, each once
- step: int32 [2], P('group'), parts along dimension 0, may hold values from 0 to 27
- q_gain: float32 [128], replicated, may hold values from 1 to 2.5
- k_gain: float32 [128], replicated, may hold values from 1 to 2.5
- gate_table: float32 [28, 1536], replicated, may hold values from 0.5 to 2
Outputs:
- attended: bfloat16 [1024, 1536], P(('group', 'patch')), parts along dimension 0
The draws below stay inside these ranges and needn't reach their ends.
There are 2 independent parts, one for each index of `group`. The reference program is written for one: setup_inputs(seed, part) draws one part's arguments, and reference() takes and returns one part's arrays. A program takes and returns all parts, laid end to end along the dimension named above; an argument that names none is the same for every part. Nothing has to cross between parts.
Inputs may be any that keep to these rules, and one draw needn't show every extreme that they name: `patch_owner`: A permutation: each patch is held by exactly one device.
All inputs are finite; a program needn't handle non-finite values.
Results may differ from the reference program's by a relative error of at most 0.009.
Values may be sent and summed in bfloat16 or wider, within the bound.
No kernel may reach another device: no remote copies, remote signals or barrier semaphores. Data moves between devices by JAX's collectives and lax.ppermute only.
A program may use at most 128 MiB of HBM per device.

```python
import jax
import jax.numpy as jnp
from jax import lax

H = 12
DH = 128
HD = 1536
TOK_DEV = 32
IMG = 512
TXT = 512
GRID_W = 64
STEPS = 28
PROMPTS = 16
N_PATCH = 16


def draw_queries(key, part):
    normal_part = jnp.clip(jax.random.normal(jax.random.fold_in(key, 1), (IMG, HD), jnp.float32), -6.0, 6.0)
    return normal_part.astype(jnp.bfloat16)


def draw_text_keys(key, part):
    normal_part = 1.5 * jnp.clip(jax.random.normal(jax.random.fold_in(key, 2), (PROMPTS, TXT, HD), jnp.float32), -6.0, 6.0)
    return normal_part.astype(jnp.bfloat16)


def block_levels(own_key, extent, cuts, least, high):
    def one(axis_at, blocks):
        heights = jax.random.uniform(jax.random.fold_in(jax.random.fold_in(own_key, 6), axis_at), (blocks,), jnp.float32, least / len(cuts), high / len(cuts))
        return jnp.repeat(jnp.exp(heights), extent[axis_at] // blocks).reshape((-1,) + (1,) * (len(extent) - axis_at - 1))

    level = one(*cuts[0])
    for cut in cuts[1:]:
        level = level * one(*cut)
    return level


def scatter_about(stream_key, dims, deviation, limit, shards=(), held_as=jnp.bfloat16):
    values = jax.random.normal(stream_key, dims, jnp.float32) * deviation
    if len(shards) > 0:
        values = block_levels(stream_key, dims, shards, -0.22, 0.18) * values
    return jnp.clip(values, min=-limit, max=limit).astype(held_as)


def setup_inputs(seed: int = 0, part: int = 0) -> dict:
    arg_keys = jax.random.split(jax.random.key(seed), 14)
    part_splits = jax.random.split(jax.random.fold_in(arg_keys[13], part), 14)
    queries = draw_queries(jax.random.fold_in(jax.random.fold_in(arg_keys[13], part), 71), part)
    keys = scatter_about(part_splits[1], (IMG, HD), 1.0, 6.0, ((0, 16),))
    values = scatter_about(part_splits[2], (IMG, HD), 1.0, 6.0, ((0, 16),))
    stale_keys = scatter_about(part_splits[3], (IMG, HD), 1.5, 6.0, ((0, 16),))
    stale_values = scatter_about(part_splits[4], (IMG, HD), 1.0, 6.0, ((0, 16),))
    text_keys = draw_text_keys(jax.random.fold_in(jax.random.fold_in(arg_keys[13], part), 71), part)
    text_values = scatter_about(part_splits[6], (PROMPTS, TXT, HD), 1.0, 6.0, ((0, 16),))
    prompt_device = jax.random.randint(part_splits[7], (1,), 0, N_PATCH).astype(jnp.int32)
    patch_owner = jax.random.permutation(part_splits[8], N_PATCH).astype(jnp.int32)
    step = jax.random.randint(part_splits[9], (1,), 0, STEPS).astype(jnp.int32)
    q_gain = jnp.clip(jax.random.uniform(arg_keys[10], (DH,), jnp.float32, 1.0, 2.5), 1.0, 2.5)
    k_gain = jnp.clip(jax.random.uniform(arg_keys[11], (DH,), jnp.float32, 1.0, 2.5), 1.0, 2.5)
    gate_table = jnp.clip(jax.random.uniform(arg_keys[12], (STEPS, HD), jnp.float32, 0.5, 2.0), 0.5, 2.0)
    return dict(queries=queries, keys=keys, values=values, stale_keys=stale_keys, stale_values=stale_values, text_keys=text_keys, text_values=text_values, prompt_device=prompt_device, patch_owner=patch_owner, step=step, q_gain=q_gain, k_gain=k_gain, gate_table=gate_table)


epsilon = 1e-06

def rms_norm(values_in, gain):
    row_count = values_in.shape[0]
    heads_in = values_in.astype(jnp.float32).reshape(row_count, -1, DH)
    mean_square = lax.optimization_barrier(jnp.mean(heads_in * heads_in, axis=-1, keepdims=True))
    return heads_in * lax.rsqrt(mean_square + epsilon) * gain

def rope_tables(grid_index):
    grid_row = (grid_index // GRID_W).astype(jnp.float32)
    grid_col = (grid_index % GRID_W).astype(jnp.float32)
    omega = 10000.0 ** (-2.0 * jnp.arange(28, dtype=jnp.float32) / 56.0)
    angle = jnp.concatenate([jnp.zeros((grid_index.shape[0], 8), jnp.float32), grid_row[:, None] * omega, grid_col[:, None] * omega], axis=1)
    return (jnp.cos(angle), jnp.sin(angle))

def rotate(normed, cosine, sine_part):
    row_count, head_count = (normed.shape[0], normed.shape[1])
    paired = normed.reshape(row_count, head_count, DH // 2, 2)
    real_part = paired[..., 0]
    imag_part = paired[..., 1]
    cos_heads = cosine[:, None, :]
    sin_heads = sine_part[:, None, :]
    rotated = jnp.stack([cos_heads * real_part - sin_heads * imag_part, sin_heads * real_part + cos_heads * imag_part], axis=-1)
    return rotated.reshape(row_count, head_count * DH).astype(jnp.bfloat16)

def reference(queries, keys, values, stale_keys, stale_values, text_keys, text_values, prompt_device, patch_owner, step, q_gain, k_gain, gate_table):
    row_ids = jnp.arange(IMG, dtype=jnp.int32)
    grid_index = patch_owner[row_ids // TOK_DEV] * TOK_DEV + row_ids % TOK_DEV
    cosine, sine_part = rope_tables(grid_index)
    query_rot = rotate(rms_norm(queries, q_gain), cosine, sine_part)
    key_rot = rotate(rms_norm(keys, k_gain), cosine, sine_part)
    text_rows = lax.dynamic_index_in_dim(text_keys, prompt_device[0], 0, keepdims=False)
    text_vals = lax.dynamic_index_in_dim(text_values, prompt_device[0], 0, keepdims=False)
    gate_row = lax.dynamic_index_in_dim(gate_table, step[0], 0, keepdims=False)

    def one_block(block_id):
        first_row = (block_id * TOK_DEV).astype(jnp.int32)
        query_block = lax.dynamic_slice_in_dim(query_rot, first_row, TOK_DEV, 0)
        own_keys = lax.dynamic_slice_in_dim(key_rot, first_row, TOK_DEV, 0)
        own_values = lax.dynamic_slice_in_dim(values, first_row, TOK_DEV, 0)
        image_keys = lax.dynamic_update_slice_in_dim(stale_keys, own_keys, first_row, 0)
        image_values = lax.dynamic_update_slice_in_dim(stale_values, own_values, first_row, 0)
        all_keys = jnp.concatenate([text_rows, image_keys], axis=0)
        all_values = jnp.concatenate([text_vals, image_values], axis=0)
        query_heads = query_block.reshape(TOK_DEV, H, DH).astype(jnp.float32)
        key_heads = all_keys.reshape(-1, H, DH).astype(jnp.float32)
        value_heads = all_values.reshape(-1, H, DH).astype(jnp.float32)
        scores = jnp.einsum('qhd,khd->hqk', query_heads, key_heads) * DH ** (-0.5)
        weights = jax.nn.softmax(scores, axis=-1).astype(jnp.bfloat16)
        mixed = jnp.einsum('hqk,khd->qhd', weights.astype(jnp.float32), value_heads)
        return (mixed.reshape(TOK_DEV, H * DH) * gate_row).astype(jnp.bfloat16)
    blocks = lax.map(one_block, jnp.arange(N_PATCH, dtype=jnp.int32))
    return blocks.reshape(IMG, H * DH)
```

```python
import functools

import jax
import jax.numpy as jnp
import numpy as np
from jax import lax
from jax.experimental import pallas as pl
from jax.experimental.pallas import tpu as pltpu
from jax.sharding import PartitionSpec as P

DH = 128
GRID_W = 64
EPSILON = 1e-06
QUAD = 4
PART = 32


F32 = jnp.float32
BF16 = jnp.bfloat16
VMEM = pl.BlockSpec(memory_space=pltpu.VMEM)
SMEM = pl.BlockSpec(memory_space=pltpu.SMEM)
ANY = pl.BlockSpec(memory_space=pl.ANY)


def swap(shard, bits):
    return lax.ppermute(shard, "patch", [(i, i ^ bits) for i in range(lax.axis_size("patch"))])


def lane_rates():
    omega = 10000.0 ** (-2.0 * np.arange(28, dtype=np.float64) / 56.0)
    rates = np.zeros((8, DH), np.float32)
    rates[0, 16:72] = np.repeat(omega, 2)
    rates[1, 72:128] = np.repeat(omega, 2)
    rates[2] = np.tile([-1.0, 1.0], DH // 2)
    return rates


def head_slices(width):
    return [slice(h * DH, (h + 1) * DH) for h in range(width // DH)]


def norm_rotate(rows, gain, cosine, sine, even):
    rows = rows.astype(F32)
    normed = rows * lax.rsqrt(jnp.mean(rows * rows, axis=-1, keepdims=True) + EPSILON) * gain
    other = jnp.where(even, pltpu.roll(normed, DH - 1, 1), pltpu.roll(normed, 1, 1))
    return (normed * cosine + other * sine).astype(BF16)


def prepare_kernel(owner, q, k, sk, sv, q_gain, k_gain, rates, q_out, k_out, kv_out):
    rows, width = q.shape
    first = owner[lax.axis_index("patch")] * rows
    token = first + lax.broadcasted_iota(jnp.int32, (rows, DH), 0)
    angle = (token // GRID_W).astype(F32) * rates[0:1, :] + (token % GRID_W).astype(F32) * rates[1:2, :]
    cosine = jnp.cos(angle)
    sine = jnp.sin(angle) * rates[2:3, :]
    even = lax.broadcasted_iota(jnp.int32, (rows, DH), 1) % 2 == 0
    for part in head_slices(width):
        q_out[:, part] = norm_rotate(q[:, part], q_gain[...], cosine, sine, even)
        k_out[:, part] = norm_rotate(k[:, part], k_gain[...], cosine, sine, even)
    kv_out[:rows] = sk[...]
    kv_out[rows:] = sv[...]


def prepare(patch_owner, queries, keys, stale_keys, stale_values, q_gain, k_gain):
    rows, width = queries.shape
    return pl.pallas_call(
        prepare_kernel,
        name="prepare",
        out_shape=(
            jax.ShapeDtypeStruct((rows, width), BF16),
            jax.ShapeDtypeStruct((rows, width), BF16),
            jax.ShapeDtypeStruct((2 * rows, width), BF16),
        ),
        in_specs=[SMEM] + [VMEM] * 7,
        out_specs=(VMEM, VMEM, VMEM),
    )(
        patch_owner, queries, keys, stale_keys, stale_values,
        q_gain.reshape(1, DH), k_gain.reshape(1, DH), jnp.asarray(lane_rates()),
    )


def attend(q, blocks, outs, width):
    total = q.shape[0]
    rows = total // len(outs)
    lane = lax.broadcasted_iota(jnp.int32, (total, DH), 1)
    logs = jnp.zeros((total, DH), F32)
    for h, part in enumerate(head_slices(width)):
        q_head = q[:, part]
        scores = [
            lax.dot_general(q_head, keys[:, part], (((1,), (1,)), ((), ())), preferred_element_type=F32)
            * DH ** (-0.5)
            for keys, _ in blocks
        ]
        highest = functools.reduce(jnp.maximum, [jnp.max(s, axis=-1, keepdims=True) for s in scores])
        weights = [jnp.exp(s - highest) for s in scores]
        sums = functools.reduce(jnp.add, [jnp.sum(w, axis=-1, keepdims=True) for w in weights])
        mixed = functools.reduce(
            jnp.add,
            [
                jnp.dot(w.astype(BF16), values[:, part], preferred_element_type=F32)
                for w, (_, values) in zip(weights, blocks)
            ],
        )
        mixed = (mixed / sums).astype(BF16)
        logs = jnp.where(lane == h, highest + jnp.log(sums), logs)
        for n, out in enumerate(outs):
            out[:, part] = mixed[n * rows : (n + 1) * rows]
    coded = encode(logs)
    for n, out in enumerate(outs):
        out[:, width:] = coded[n * rows : (n + 1) * rows]


def encode(logs):
    high = logs.astype(BF16).astype(F32)
    middle = (logs - high).astype(BF16).astype(F32)
    low = logs - high - middle
    return (high + pltpu.roll(middle, PART, 1) + pltpu.roll(low, 2 * PART, 1)).astype(BF16)


def decode(coded):
    coded = coded.astype(F32)
    return coded + pltpu.roll(coded, DH - PART, 1) + pltpu.roll(coded, DH - 2 * PART, 1)


def fetch_text(own, refs, buffers, sem):
    text_k, text_v, other_k, other_v = refs

    def copies(sources):
        return [pltpu.make_async_copy(s, b, sem.at[n]) for n, (s, b) in enumerate(zip(sources, buffers))]

    @pl.when(own)
    def _():
        for c in copies((text_k, text_v)):
            c.start()

    @pl.when(jnp.logical_not(own))
    def _():
        for c in copies((other_k, other_v)):
            c.start()

    return copies((text_k, text_v))


def text_kernel(pieces, prompt, *refs):
    q = refs[:pieces]
    text = refs[pieces : pieces + 4]
    outs = refs[pieces + 4 : 2 * pieces + 4]
    q_all, key_buf, value_buf, sem = refs[2 * pieces + 4 :]
    rows, width = q[0].shape
    me = lax.axis_index("patch")

    @pl.when(me // 2 == prompt[0] // 2)
    def _():
        waits = fetch_text(me == prompt[0], text, (key_buf, value_buf), sem)
        for n in range(pieces):
            q_all[n * rows : (n + 1) * rows] = q[n][...]
        for w in waits:
            w.wait()
        attend(q_all, [(key_buf, value_buf)], outs, width)


def text_attention(prompt, pieces, text):
    rows, width = pieces[0].shape
    count = len(pieces)
    keys = text[0].shape
    return pl.pallas_call(
        functools.partial(text_kernel, count),
        name="text",
        out_shape=[jax.ShapeDtypeStruct((rows, width + DH), BF16)] * count,
        in_specs=[SMEM] + [VMEM] * count + [ANY] * 4,
        out_specs=[VMEM] * count,
        scratch_shapes=[
            pltpu.VMEM((count * rows, width), BF16),
            pltpu.VMEM(keys, BF16),
            pltpu.VMEM(keys, BF16),
            pltpu.SemaphoreType.DMA((2,)),
        ],
    )(prompt, *pieces, *text)


def line_kernel(pieces, fresh, prompt, *refs):
    q = refs[:pieces]
    kv = refs[pieces : pieces + QUAD]
    text = refs[pieces + QUAD : pieces + QUAD + 4]
    refs = refs[pieces + QUAD + 4 :]
    if fresh:
        k_rot, values = refs[:2]
        refs = refs[2:]
    outs = refs[:pieces]
    q_all, k_all, v_all, key_buf, value_buf, sem = refs[pieces:]
    rows, width = q[0].shape
    me = lax.axis_index("patch")
    here = me // 2 == prompt[0] // 2
    for n in range(pieces):
        q_all[n * rows : (n + 1) * rows] = q[n][...]
    for n in range(QUAD):
        span = slice(n * rows, (n + 1) * rows)
        if fresh and n == 0:
            k_all[span] = k_rot[...]
            v_all[span] = values[...]
        else:
            k_all[span] = kv[n][:rows]
            v_all[span] = kv[n][rows:]

    @pl.when(here)
    def _():
        for w in fetch_text(me == prompt[0], text, (key_buf, value_buf), sem):
            w.wait()
        attend(q_all, [(k_all, v_all), (key_buf, value_buf)], outs, width)

    @pl.when(jnp.logical_not(here))
    def _():
        attend(q_all, [(k_all, v_all)], outs, width)


def line_attention(prompt, pieces, kv, text, fresh=()):
    rows, width = pieces[0].shape
    count = len(pieces)
    keys = text[0].shape
    return pl.pallas_call(
        functools.partial(line_kernel, count, bool(fresh)),
        name="line",
        out_shape=[jax.ShapeDtypeStruct((rows, width + DH), BF16)] * count,
        in_specs=[SMEM] + [VMEM] * (count + QUAD) + [ANY] * 4 + [VMEM] * len(fresh),
        out_specs=[VMEM] * count,
        scratch_shapes=[
            pltpu.VMEM((count * rows, width), BF16),
            pltpu.VMEM((QUAD * rows, width), BF16),
            pltpu.VMEM((QUAD * rows, width), BF16),
            pltpu.VMEM(keys, BF16),
            pltpu.VMEM(keys, BF16),
            pltpu.SemaphoreType.DMA((2,)),
        ],
    )(prompt, *pieces, *kv, *text, *fresh)


def weigh(sources):
    logs = [decode(log) if valid is None else jnp.where(valid, decode(log), -1e30) for log, valid in sources]
    highest = functools.reduce(jnp.maximum, logs)
    weights = [jnp.exp(log - highest) for log in logs]
    total = functools.reduce(jnp.add, weights)
    lane = lax.broadcasted_iota(jnp.int32, total.shape, 1)
    logs = jnp.where(lane < PART, highest + jnp.log(total), 0.0)
    return [w / total for w in weights], logs


def blend(shares, sources, h, part):
    terms = []
    for share, (ref, valid) in zip(shares, sources):
        mean = ref[:, part].astype(F32)
        if valid is not None:
            mean = jnp.where(valid, mean, 0.0)
        terms.append(share[:, h : h + 1] * mean)
    return functools.reduce(jnp.add, terms)


def merge_kernel(pieces, prompt, *refs):
    near, back, outs = refs[:pieces], refs[pieces : 2 * pieces], refs[2 * pieces :]
    width = near[0].shape[1] - DH
    across = lax.axis_index("patch") // 2 == (prompt[0] // 2) ^ 1

    @pl.when(across)
    def _():
        for a, b, out in zip(near, back, outs):
            shares, logs = weigh([(a[:, width:], None), (b[:, width:], None)])
            for h, part in enumerate(head_slices(width)):
                out[:, part] = blend(shares, [(a, None), (b, None)], h, part).astype(BF16)
            out[:, width:] = encode(logs)

    @pl.when(jnp.logical_not(across))
    def _():
        for a, out in zip(near, outs):
            out[...] = a[...]


def merge(prompt, near, back):
    count = len(near)
    return pl.pallas_call(
        functools.partial(merge_kernel, count),
        name="merge",
        out_shape=[jax.ShapeDtypeStruct(x.shape, BF16) for x in near],
        in_specs=[SMEM] + [VMEM] * (2 * count),
        out_specs=[VMEM] * count,
    )(prompt, *near, *back)


def finish_kernel(prompt, step, gate_table, own, back, *refs):
    got, (out, gate, sem) = refs[:-3], refs[-3:]
    width = out.shape[1]
    fetch = pltpu.make_async_copy(gate_table.at[pl.ds(step[0], 1)], gate, sem)
    fetch.start()
    across = lax.axis_index("patch") // 2 == (prompt[0] // 2) ^ 1
    sources = [(own, None), (back, across)] + [(g, None) for g in got]
    shares, _ = weigh([(ref[:, width:], valid) for ref, valid in sources])
    fetch.wait()
    for h, part in enumerate(head_slices(width)):
        out[:, part] = (blend(shares, sources, h, part) * gate[:, part]).astype(BF16)


def finish(prompt, step, gate_table, own, back, got):
    rows, width = own.shape
    return pl.pallas_call(
        finish_kernel,
        name="finish",
        out_shape=jax.ShapeDtypeStruct((rows, width - DH), BF16),
        in_specs=[SMEM, SMEM, ANY] + [VMEM] * (2 + len(got)),
        out_specs=VMEM,
        scratch_shapes=[pltpu.VMEM((1, width - DH), F32), pltpu.SemaphoreType.DMA],
    )(prompt, step, gate_table, own, back, *got)


def grouped(call, *lists):
    out = []
    for n in range(0, len(lists[0]), 4):
        out += call(*[x[n : n + 4] for x in lists])
    return out


def local(
    queries,
    keys,
    values,
    stale_keys,
    stale_values,
    text_keys,
    text_values,
    prompt_device,
    patch_owner,
    step,
    q_gain,
    k_gain,
    gate_table,
):
    length = lax.axis_size("patch") // QUAD
    q_rot, k_rot, kv = prepare(patch_owner, queries, keys, stale_keys, stale_values, q_gain, k_gain)
    q_line = [q_rot] + [swap(q_rot, QUAD * d) for d in range(1, length)]
    q_other = [swap(q, 2) for q in q_line]
    kv_y = swap(kv, 2)
    kv_quad = [kv, swap(kv, 1), kv_y, swap(kv_y, 1)]
    text = [text_keys[0], text_values[0]]
    text += [swap(t, 1) for t in text]
    other = grouped(lambda q: text_attention(prompt_device, q, text), q_other)
    back = [swap(t, 2) for t in other]
    own = line_attention(prompt_device, q_line[:1], kv_quad, text, (k_rot, values))
    near = grouped(lambda q: line_attention(prompt_device, q, kv_quad, text), q_line[1:])
    merged = grouped(lambda a, b: merge(prompt_device, a, b), near, back[1:])
    got = [swap(m, QUAD * (d + 1)) for d, m in enumerate(merged)]
    return finish(prompt_device, step, gate_table, own[0], back[0], got)


def solution(mesh):
    return jax.shard_map(
        local,
        mesh=mesh,
        in_specs=(
            P(("group", "patch"), None),
            P(("group", "patch"), None),
            P(("group", "patch"), None),
            P(("group", "patch"), None),
            P(("group", "patch"), None),
            P(("group", "patch"), None, None),
            P(("group", "patch"), None, None),
            P("group"),
            P("group"),
            P("group"),
            P(),
            P(),
            P(),
        ),
        out_specs=P(("group", "patch"), None),
        check_vma=False,
    )
```

```python
import functools

import jax
import jax.numpy as jnp
import numpy as np
from jax import lax
from jax.experimental import pallas as pl
from jax.experimental.pallas import tpu as pltpu
from jax.sharding import PartitionSpec as P


DH = 128
GRID_W = 64
EPSILON = 1e-06
QUAD = 4
LOG2E = 1.4426950408889634
PART = 32


F32 = jnp.float32
BF16 = jnp.bfloat16
VMEM = pl.BlockSpec(memory_space=pltpu.VMEM)
SMEM = pl.BlockSpec(memory_space=pltpu.SMEM)
ANY = pl.BlockSpec(memory_space=pl.ANY)
HBM = pl.BlockSpec(memory_space=pltpu.HBM)


def swap(shard, bits):
    return lax.ppermute(shard, "patch", [(i, i ^ bits) for i in range(lax.axis_size("patch"))])


def in_hbm(x):
    return pltpu.with_memory_space_constraint(x, pltpu.HBM)


def lane_rates():
    omega = 10000.0 ** (-2.0 * np.arange(28, dtype=np.float64) / 56.0)
    rates = np.zeros((8, DH), np.float32)
    rates[0, 16:72] = np.repeat(omega, 2)
    rates[1, 72:128] = np.repeat(omega, 2)
    rates[2] = np.tile([-1.0, 1.0], DH // 2)
    return rates


def head_slices(width):
    return [slice(h * DH, (h + 1) * DH) for h in range(width // DH)]


def norm_rotate(rows, gain, cosine, sine, out):
    parts = head_slices(rows.shape[1])
    even = lax.broadcasted_iota(jnp.int32, cosine.shape, 1) % 2 == 0
    heads = [rows[:, part].astype(F32) for part in parts]
    squares = [jnp.mean(x * x, axis=-1, keepdims=True) for x in heads]
    normed = [x * lax.rsqrt(square + EPSILON) * gain for x, square in zip(heads, squares)]
    other = [jnp.where(even, pltpu.roll(x, DH - 1, 1), pltpu.roll(x, 1, 1)) for x in normed]
    rotated = [(x * cosine + y * sine).astype(BF16) for x, y in zip(normed, other)]
    for part, x in zip(parts, rotated):
        out[:, part] = x


def gather_queries(pieces, first, gain, cosine, sine, out):
    rows = pieces[0].shape[0]
    for n, (piece, row) in enumerate(zip(pieces, first)):
        span = slice(row, row + rows)
        norm_rotate(piece, gain[...], cosine[span], sine[span], out.at[n * rows : (n + 1) * rows])


def prepare_kernel(owner, *refs):
    sources, (q_out, k_out, kv_out, v_out, cosine, sine, gain_out, q, k, k_gain, rates, sem) = refs[:8], refs[8:]
    rows, _ = q.shape
    targets = [rates, gain_out, q, k_gain, k, kv_out.at[:rows], kv_out.at[rows:], v_out]
    copies = [pltpu.make_async_copy(s, t, sem.at[n]) for n, (s, t) in enumerate(zip(sources, targets))]
    for c in copies:
        c.start()
    me = lax.axis_index("patch")
    length = owner.shape[0] // QUAD
    copies[0].wait()
    for slot in range(2 * length):
        first = owner[me ^ (2 * (slot // length)) ^ (QUAD * (slot % length))] * rows
        token = first + lax.broadcasted_iota(jnp.int32, (rows, DH), 0)
        angle = (token // GRID_W).astype(F32) * rates[0:1, :] + (token % GRID_W).astype(F32) * rates[1:2, :]
        cosine[slot * rows : (slot + 1) * rows] = jnp.cos(angle)
        sine[slot * rows : (slot + 1) * rows] = jnp.sin(angle) * rates[2:3, :]
    for c in copies[1:]:
        c.wait()
    norm_rotate(q, gain_out[...], cosine[:rows], sine[:rows], q_out)
    norm_rotate(k, k_gain[...], cosine[:rows], sine[:rows], k_out)


def prepare(patch_owner, queries, keys, values, stale_keys, stale_values, q_gain, k_gain):
    rows, width = queries.shape
    rates = jnp.asarray(lane_rates())
    table = jax.ShapeDtypeStruct((patch_owner.shape[0] // 2 * rows, DH), F32)
    return pl.pallas_call(
        prepare_kernel,
        name="prepare",
        out_shape=(
            jax.ShapeDtypeStruct((rows, width), BF16),
            jax.ShapeDtypeStruct((rows, width), BF16),
            jax.ShapeDtypeStruct((2 * rows, width), BF16),
            jax.ShapeDtypeStruct((rows, width), BF16),
            table,
            table,
            jax.ShapeDtypeStruct((1, DH), F32),
        ),
        in_specs=[SMEM] + [HBM] * 8,
        out_specs=(VMEM,) * 7,
        scratch_shapes=[
            pltpu.VMEM((rows, width), BF16),
            pltpu.VMEM((rows, width), BF16),
            pltpu.VMEM((1, DH), F32),
            pltpu.VMEM(rates.shape, F32),
            pltpu.SemaphoreType.DMA((8,)),
        ],
        compiler_params=pltpu.CompilerParams(vmem_limit_bytes=8 * 2**20),
    )(
        in_hbm(patch_owner),
        *[
            in_hbm(x)
            for x in (
                rates, q_gain.reshape(1, DH), queries,
                k_gain.reshape(1, DH), keys, stale_keys, stale_values, values,
            )
        ],
    )


def attend(q, blocks, outs, width, scores, weights):
    total = q.shape[0]
    rows = total // len(outs)
    parts = head_slices(width)
    spans, keys = [], 0
    for block in blocks:
        spans.append(slice(keys, keys + block[0].shape[0]))
        keys = spans[-1].stop
    for block, span in zip(blocks, spans):
        for h, part in enumerate(parts):
            scores[h, :, span] = lax.dot_general(
                q[:, part], block[0][:, part], (((1,), (1,)), ((), ())), preferred_element_type=F32
            ) * (DH ** (-0.5) * LOG2E)
    lane = lax.broadcasted_iota(jnp.int32, (total, DH), 1)
    logs = jnp.zeros((total, DH), F32)
    step = max(1, min(len(parts), 65536 // (total * keys)))
    for first in range(0, len(parts), step):
        some = slice(first, min(first + step, len(parts)))
        score = scores[some, :, :keys]
        highest = jnp.max(score, axis=-1, keepdims=True)
        weight = jnp.exp2(score - highest)
        mass = jnp.sum(weight, axis=-1, keepdims=True)
        weights[some, :, :keys] = (weight * (1.0 / mass)).astype(BF16)
        log = highest + jnp.log2(mass)
        for h in range(some.start, some.stop):
            logs = jnp.where(lane == h, log[h - first], logs)
    mixed = [
        functools.reduce(
            jnp.add,
            [
                jnp.dot(weights[h, :, span], block[1][:, part], preferred_element_type=F32)
                for block, span in zip(blocks, spans)
            ],
        ).astype(BF16)
        for h, part in enumerate(parts)
    ]
    coded = encode(logs)
    for n, out in enumerate(outs):
        mine = slice(n * rows, (n + 1) * rows)
        for h, part in enumerate(parts):
            out[:, part] = mixed[h][mine]
        out[:, width:] = coded[mine]


def encode(logs):
    high = logs.astype(BF16).astype(F32)
    middle = (logs - high).astype(BF16).astype(F32)
    low = logs - high - middle
    return (high + pltpu.roll(middle, PART, 1) + pltpu.roll(low, 2 * PART, 1)).astype(BF16)


def decode(coded):
    coded = coded.astype(F32)
    return coded + pltpu.roll(coded, DH - PART, 1) + pltpu.roll(coded, DH - 2 * PART, 1)


def fetch_kernel(first, prompt, gain, cosine, sine, *refs):
    pieces = len(first)
    q = refs[:pieces]
    sources = refs[pieces : pieces + 4]
    outs = refs[pieces + 4 : 2 * pieces + 4]
    *text, q_all, scores, weights, sem = refs[2 * pieces + 4 :]
    me = lax.axis_index("patch")

    def copies(held):
        return [pltpu.make_async_copy(s, t, sem.at[n]) for n, (s, t) in enumerate(zip(held, text))]

    @pl.when(me // 2 == prompt[0] // 2)
    def _():
        @pl.when(me == prompt[0])
        def _():
            for c in copies(sources[:2]):
                c.start()

        @pl.when(me != prompt[0])
        def _():
            for c in copies(sources[2:]):
                c.start()

        gather_queries(q, first, gain, cosine, sine, q_all)
        for c in copies(sources[:2]):
            c.wait()
        attend(q_all, [tuple(text)], outs, q_all.shape[1], scores, weights)


def text_kernel(first, prompt, gain, cosine, sine, *refs):
    pieces = len(first)
    q = refs[:pieces]
    text = refs[pieces : pieces + 2]
    outs = refs[pieces + 2 : 2 * pieces + 2]
    q_all, scores, weights = refs[2 * pieces + 2 :]

    @pl.when(lax.axis_index("patch") // 2 == prompt[0] // 2)
    def _():
        gather_queries(q, first, gain, cosine, sine, q_all)
        attend(q_all, [text], outs, q_all.shape[1], scores, weights)


def text_attention(prompt, tables, pieces, first, text):
    rows, width = pieces[0].shape
    count = len(pieces)
    keys = text[0].shape
    fetch = len(text) == 4
    return pl.pallas_call(
        functools.partial(fetch_kernel if fetch else text_kernel, first),
        name="fetch" if fetch else "text",
        out_shape=[jax.ShapeDtypeStruct((rows, width + DH), BF16)] * count
        + [jax.ShapeDtypeStruct(keys, BF16)] * (2 * fetch),
        in_specs=[SMEM] + [VMEM] * (3 + count) + ([ANY] * 4 if fetch else [VMEM] * 2),
        out_specs=[VMEM] * (count + 2 * fetch),
        scratch_shapes=[
            pltpu.VMEM((count * rows, width), BF16),
            pltpu.VMEM((width // DH, count * rows, keys[0]), F32),
            pltpu.VMEM((width // DH, count * rows, keys[0]), BF16),
        ]
        + [pltpu.SemaphoreType.DMA((2,))] * fetch,
        compiler_params=pltpu.CompilerParams(vmem_limit_bytes=16 * 2**20),
    )(prompt, *tables, *pieces, *text)


def line_kernel(first, prompt, *refs):
    own = first is None
    if not own:
        (gain, cosine, sine), refs = refs[:3], refs[3:]
    pieces = 1 if own else len(first)
    q = refs[:pieces]
    rows, width = q[0].shape
    kv, kv_c, *far = refs[pieces : pieces + 6]
    quad_k = [kv.at[:rows], kv_c.at[:rows]] + far[::2]
    quad_v = [kv.at[rows:], kv_c.at[rows:]] + far[1::2]
    text = refs[pieces + 6 : pieces + 8]
    refs = refs[pieces + 8 :]
    if own:
        (quad_k[0], quad_v[0], step, gate_table), refs = refs[:4], refs[4:]
        out, gate, *refs, sem = refs
        refs = [out, *refs]
        read_gate = pltpu.make_async_copy(gate_table.at[pl.ds(step[0], 1)], gate, sem)
        read_gate.start()
    outs = refs[:pieces]
    q_all, k_all, v_all, scores, weights = refs[pieces:]
    if own:
        q_all[...] = q[0][...]
    else:
        gather_queries(q, first, gain, cosine, sine, q_all)
    for n in range(QUAD):
        k_all[n * rows : (n + 1) * rows] = quad_k[n][...]
        v_all[n * rows : (n + 1) * rows] = quad_v[n][...]
    here = lax.axis_index("patch") // 2 == prompt[0] // 2

    @pl.when(here)
    def _():
        attend(q_all, [(k_all, v_all), text], outs, width, scores, weights)

    @pl.when(jnp.logical_not(here))
    def _():
        attend(q_all, [(k_all, v_all)], outs, width, scores, weights)

    if own:
        read_gate.wait()


def line_attention(prompt, tables, pieces, first, kv, text, fresh=()):
    rows, width = pieces[0].shape
    count = len(pieces)
    every = text[0].shape[0] + QUAD * rows
    return pl.pallas_call(
        functools.partial(line_kernel, first),
        name="own" if fresh else "line",
        out_shape=[jax.ShapeDtypeStruct((rows, width + DH), BF16)] * count
        + [jax.ShapeDtypeStruct((1, width), F32)] * bool(fresh),
        in_specs=[SMEM] + [VMEM] * (len(tables) + count + 8) + [VMEM, VMEM, SMEM, HBM] * bool(fresh),
        out_specs=[VMEM] * (count + bool(fresh)),
        scratch_shapes=[
            pltpu.VMEM((count * rows, width), BF16),
            pltpu.VMEM((QUAD * rows, width), BF16),
            pltpu.VMEM((QUAD * rows, width), BF16),
            pltpu.VMEM((width // DH, count * rows, every), F32),
            pltpu.VMEM((width // DH, count * rows, every), BF16),
        ]
        + [pltpu.SemaphoreType.DMA] * bool(fresh),
        compiler_params=pltpu.CompilerParams(vmem_limit_bytes=16 * 2**20),
    )(prompt, *tables, *pieces, *kv, *text, *fresh)


def weigh(sources):
    logs = [decode(log) if valid is None else jnp.where(valid, decode(log), -1e30) for log, valid in sources]
    highest = functools.reduce(jnp.maximum, logs)
    weights = [jnp.exp2(log - highest) for log in logs]
    total = functools.reduce(jnp.add, weights)
    lane = lax.broadcasted_iota(jnp.int32, total.shape, 1)
    logs = jnp.where(lane < PART, highest + jnp.log2(total), 0.0)
    return [w / total for w in weights], logs


def blend(shares, sources, h, part):
    terms = []
    for share, (ref, valid) in zip(shares, sources):
        mean = ref[:, part].astype(F32)
        if valid is not None:
            mean = jnp.where(valid, mean, 0.0)
        terms.append(share[:, h : h + 1] * mean)
    return functools.reduce(jnp.add, terms)


def merge_kernel(pieces, prompt, *refs):
    near, back, outs = refs[:pieces], refs[pieces : 2 * pieces], refs[2 * pieces :]
    width = near[0].shape[1] - DH
    across = lax.axis_index("patch") // 2 == (prompt[0] // 2) ^ 1

    @pl.when(across)
    def _():
        for a, b, out in zip(near, back, outs):
            shares, logs = weigh([(a[:, width:], None), (b[:, width:], None)])
            for h, part in enumerate(head_slices(width)):
                out[:, part] = blend(shares, [(a, None), (b, None)], h, part).astype(BF16)
            out[:, width:] = encode(logs)

    @pl.when(jnp.logical_not(across))
    def _():
        for a, out in zip(near, outs):
            out[...] = a[...]


def merge(prompt, near, back):
    count = len(near)
    return pl.pallas_call(
        functools.partial(merge_kernel, count),
        name="merge",
        out_shape=[jax.ShapeDtypeStruct(x.shape, BF16) for x in near],
        in_specs=[SMEM] + [VMEM] * (2 * count),
        out_specs=[VMEM] * count,
        compiler_params=pltpu.CompilerParams(vmem_limit_bytes=4 * 2**20),
    )(prompt, *near, *back)


def finish_kernel(prompt, gate, own, back, *refs):
    got, out = refs[:-1], refs[-1]
    width = out.shape[1]
    across = lax.axis_index("patch") // 2 == (prompt[0] // 2) ^ 1
    sources = [(own, None), (back, across)] + [(g, None) for g in got]
    shares, _ = weigh([(ref[:, width:], valid) for ref, valid in sources])
    for h, part in enumerate(head_slices(width)):
        out[:, part] = (blend(shares, sources, h, part) * gate[:, part]).astype(BF16)


def finish(prompt, gate, own, back, got):
    rows, width = own.shape
    return pl.pallas_call(
        finish_kernel,
        name="finish",
        out_shape=jax.ShapeDtypeStruct((rows, width - DH), BF16),
        in_specs=[SMEM] + [VMEM] * (3 + len(got)),
        out_specs=VMEM,
        compiler_params=pltpu.CompilerParams(vmem_limit_bytes=4 * 2**20),
    )(prompt, gate, own, back, *got)


def groups_of(length):
    if length == 1:
        return [[0]]
    far = list(range(length - 1, 1, -1))
    size = max(1, min(4, length // 4))
    return [[0, 1]] + [far[n : n + size] for n in range(0, len(far), size)]


def local(
    queries,
    keys,
    values,
    stale_keys,
    stale_values,
    text_keys,
    text_values,
    prompt_device,
    patch_owner,
    step,
    q_gain,
    k_gain,
    gate_table,
):
    length = lax.axis_size("patch") // QUAD
    groups = groups_of(length)
    rows = queries.shape[0]
    q_line = {0: queries}
    for d in sum(groups, []):
        if d:
            q_line[d] = swap(queries, QUAD * d)
    q_rot, k_rot, kv, v_own, cosine, sine, gain = prepare(
        patch_owner, queries, keys, values, stale_keys, stale_values, q_gain, k_gain
    )
    tables = (gain, cosine, sine)
    across = [swap(stale_keys, 2), swap(stale_values, 2)]
    kv_quad = [kv, swap(kv, 1)] + across + [swap(x, 1) for x in across]
    text = [in_hbm(text_keys[0]), in_hbm(text_values[0])]
    text += [swap(t, 1) for t in (text_keys[0], text_values[0])]
    back, got = {}, []
    for n, group in enumerate(groups):
        q_other = [swap(q_line[d], 2) for d in group]
        first = [(length + d) * rows for d in group]
        other = text_attention(prompt_device, tables, q_other, first, text)
        if n == 0:
            other, text = other[: len(group)], other[len(group) :]
            own, gate = line_attention(
                prompt_device, (), [q_rot], None, kv_quad, text, (k_rot, v_own, step, in_hbm(gate_table))
            )
        for d, t in zip(group, other):
            back[d] = swap(t, 2)
        far = [d for d in group if d]
        if far:
            first = [d * rows for d in far]
            near = line_attention(prompt_device, tables, [q_line[d] for d in far], first, kv_quad, text)
            merged = merge(prompt_device, near, [back[d] for d in far])
            got += [swap(m, QUAD * d) for d, m in zip(far, merged)]
    return finish(prompt_device, gate, own, back[0], got)


def solution(mesh):
    return jax.shard_map(
        local,
        mesh=mesh,
        in_specs=(
            P(("group", "patch"), None),
            P(("group", "patch"), None),
            P(("group", "patch"), None),
            P(("group", "patch"), None),
            P(("group", "patch"), None),
            P(("group", "patch"), None, None),
            P(("group", "patch"), None, None),
            P("group"),
            P("group"),
            P("group"),
            P(),
            P(),
            P(),
        ),
        out_specs=P(("group", "patch"), None),
        check_vma=False,
    )
```
